512 devices in a mesh: user: 64 (over y, x, z_hi, core), isec: 8 (over z_lo).
Axes of the slice: x: 4, y: 4, z: 16 (z_hi: 2, z_lo: 8; z = z_hi * 8 + z_lo), core: 2. Of those that a mesh axis runs over, the one named last changes fastest.
Arguments:
- user_factors: float32 [32768, 512], P('user'), may hold values from -1.5 to 1.5
- item_factors: float32 [131072, 512], P(('user', 'isec')), may hold values from -1.5 to 1.5
- confidence: bfloat16 [64, 8, 4, 6, 128, 128], P('user', 'isec'), may hold values from 0.19921875 to 5
- tile_ids: int32 [64, 8, 4, 6], P('user', 'isec'), may hold values from 0 to 7, as said below
- tile_counts: int32 [64, 8, 4], P('user', 'isec'), may hold values from 1 to 6, as said below
Outputs:
- new_user_factors: float32 [32768, 512], P(('user', 'isec'))
- new_item_factors: float32 [131072, 512], P(('user', 'isec'))
The draws below stay inside these ranges and needn't reach their ends.
Inputs may be any that keep to these rules, and one draw needn't show every extreme that they name: `tile_ids`: the 6 positions of one list name different tiles. `tile_counts`: some list has all 6 positions live.
All inputs are finite; a program needn't handle non-finite values.
Results may differ from the reference program's by a relative error of at most 0.0003.
Values sent between devices are 32-bit elements; how exact they have to be, the bound alone decides.
A program may use at most 64 MiB of HBM per device.

```python
import math
import jax
import jax.numpy as jnp
from jax import lax

RANK = 512
TILE = 128
USER_DEV = 512
ITEM_BLOCK = 256
TILES = 6
VISITS = 4
USERS = 32768
ITEMS = 131072
N_USER = 64
N_ISEC = 8


def draw_tile_ids(key, part):
    pair_count = USER_DEV // TILE * (ITEM_BLOCK // TILE)
    scores = jax.random.randint(key, (N_USER, N_ISEC, VISITS, pair_count), 0, 1 << 20) * pair_count + jnp.arange(pair_count, dtype=jnp.int32)
    ranking = jnp.argsort(scores, axis=-1, stable=True).astype(jnp.int32)
    return ranking[..., :TILES]


def draw_tile_counts(key, part):
    base_key, bias_key, spot_key = jax.random.split(jax.random.fold_in(key, 7), 3)
    base_counts = jax.random.randint(base_key, (N_USER, N_ISEC, VISITS), 1, TILES + 1)
    owner_bias = jax.random.randint(bias_key, (N_USER, 1, 1), -2, 3)
    counts_all = jnp.clip(base_counts + owner_bias, 1, TILES)
    total_lists = N_USER * N_ISEC * VISITS
    forced_spot = jax.random.randint(spot_key, (), 0, total_lists)
    flat_counts = counts_all.reshape(total_lists)
    flat_counts = jnp.where(jnp.arange(total_lists, dtype=jnp.int32) == forced_spot, TILES, flat_counts)
    return flat_counts.reshape(N_USER, N_ISEC, VISITS).astype(jnp.int32)


def block_scale(stream_key, extent, cuts, smallest, largest):
    factor_of = 1.0
    for axis_at, blocks in cuts:
        steps = jax.random.uniform(jax.random.fold_in(jax.random.fold_in(stream_key, 6), axis_at), (blocks,), jnp.float32, smallest / len(cuts), largest / len(cuts))
        factor_of = factor_of * jnp.repeat(jnp.exp(steps), extent[axis_at] // blocks).reshape((-1,) + (1,) * (len(extent) - 1 - axis_at))
    return factor_of


def normal_values(own_key, extent, spread, most, cuts=(), kind=jnp.bfloat16):
    drawn = jax.random.normal(own_key, extent, jnp.float32) * spread
    if len(cuts) > 0:
        drawn = block_scale(own_key, extent, cuts, -0.22, 0.18) * drawn
    return jnp.clip(drawn, min=-most, max=most).astype(kind)


def setup_inputs(seed: int = 0) -> dict:
    arg_keys = jax.random.split(jax.random.key(seed), 6)
    return {
        "user_factors": normal_values(arg_keys[0], (USERS, RANK), 0.25, 1.5, ((0, 64),), jnp.float32),
        "item_factors": normal_values(arg_keys[1], (ITEMS, RANK), 0.25, 1.5, ((0, 512),), jnp.float32),
        "confidence": jnp.clip(jnp.exp(math.log(5.0) - 3.2227897 * jax.random.uniform(arg_keys[2], (N_USER, N_ISEC, VISITS, TILES, TILE, TILE), jnp.float32) ** block_scale(arg_keys[2], (N_USER, N_ISEC, VISITS, TILES, TILE, TILE), ((0, 64), (1, 8)), -0.2, 0.2)), 0.19921875, 5.0).astype(jnp.bfloat16),
        "tile_ids": draw_tile_ids(jax.random.fold_in(arg_keys[5], 71), 0),
        "tile_counts": draw_tile_counts(jax.random.fold_in(arg_keys[5], 71), 0),
    }


item_rate = 0.02
user_rate = 0.005
shrinkage = 0.1


def visit_update(owner_tiles, item_tiles, weights, indices, limit):
    highest = lax.Precision.HIGHEST
    user_count = owner_tiles.shape[0]
    item_count = item_tiles.shape[0]
    tile_total = indices.shape[0]
    pick_user = (indices[:, None] // item_count == jnp.arange(user_count, dtype=jnp.int32)[None, :]).astype(jnp.float32)
    pick_item = (indices[:, None] % item_count == jnp.arange(item_count, dtype=jnp.int32)[None, :]).astype(jnp.float32)
    chosen_users = jnp.einsum("tu,uar->tar", pick_user, owner_tiles, precision=highest)
    chosen_items = jnp.einsum("tj,jbr->tbr", pick_item, item_tiles, precision=highest)
    predicted = jnp.einsum("tar,tbr->tab", chosen_users, chosen_items, precision=highest)
    live_mask = jnp.arange(tile_total, dtype=jnp.int32) < limit
    errors = jnp.where(live_mask[:, None, None], weights.astype(jnp.float32) * (predicted - 1.0), 0.0)
    item_grad = jnp.einsum("tab,tar->tbr", errors, chosen_users, precision=highest)
    item_step = jnp.einsum("tj,tbr->jbr", pick_item, item_grad, precision=highest)
    user_grad = jnp.einsum("tab,tbr->tar", errors, chosen_items, precision=highest)
    user_step = jnp.einsum("tu,tar->uar", pick_user, user_grad, precision=highest)
    new_items = item_tiles - item_rate * (item_step + shrinkage * item_tiles)
    return new_items, user_step


def reference(user_factors, item_factors, confidence, tile_ids, tile_counts):
    user_tile_count = USER_DEV // TILE
    item_tile_count = ITEM_BLOCK // TILE
    user_tiles = user_factors.reshape(N_USER, user_tile_count, TILE, RANK)
    blocks = item_factors.reshape(N_USER, N_ISEC, item_tile_count, TILE, RANK)
    user_total = jnp.zeros((N_USER, user_tile_count, TILE, RANK), jnp.float32)

    def one_owner(packed):
        owner_tiles, owner_blocks, owner_weights, owner_ids, owner_counts = packed
        section_update = jax.vmap(visit_update, in_axes=(None, 0, 0, 0, 0))
        new_blocks, steps = section_update(owner_tiles, owner_blocks, owner_weights, owner_ids, owner_counts)
        return new_blocks, jnp.sum(steps, axis=0)

    for visit in range(VISITS):
        current = jnp.roll(blocks, visit, axis=0)
        new_blocks, steps = lax.map(one_owner, (user_tiles, current, confidence[:, :, visit], tile_ids[:, :, visit], tile_counts[:, :, visit]))
        blocks = jnp.roll(new_blocks, -visit, axis=0)
        user_total = user_total + steps
    gradient = user_total.reshape(USERS, RANK)
    new_users = user_factors - user_rate * (gradient + shrinkage * user_factors)
    return new_users, blocks.reshape(ITEMS, RANK)
```

```python
import functools

import jax
import jax.numpy as jnp
from jax import lax
from jax.experimental import pallas as pl
from jax.experimental.pallas import tpu as pltpu
from jax.sharding import PartitionSpec as P

TILE = 128
VISITS = 4

item_rate = 0.02
user_rate = 0.005
shrinkage = 0.1

MESH = pl.DeviceIdType.MESH
F32 = jnp.float32
BF16 = jnp.bfloat16


def halves(value):
    high = value.astype(BF16)
    low = (value - high.astype(F32)).astype(BF16)
    return high, low


def dot3(left, right, dims):
    one = functools.partial(
        lax.dot_general, dimension_numbers=(dims, ((), ())), preferred_element_type=F32
    )
    return one(left[0], right[0]) + (one(left[0], right[1]) + one(left[1], right[0]))


def kernel(
    n_user, n_isec,
    ids_ref, counts_ref, p_hbm, q_hbm, c_hbm,
    users_ref, items_ref,
    p_v, p_hi, p_lo, q_in, q_out, q_hi, q_lo, c_v, et_hi, et_lo, e_hi, e_lo,
    g_v, g_peer, runs, fin_out, fin_in,
    load_sem, send_sem, recv_sem, g_send, g_recv, run_send, run_recv, fin_send, fin_recv,
):
    user_rows, rank = p_v.shape
    block = q_in.shape[1]
    user_tiles = user_rows // TILE
    item_tiles = block // TILE
    share = user_rows // n_isec
    last = n_isec - 1

    u = lax.axis_index("user")
    s = lax.axis_index("isec")
    core = lax.rem(u, 2)
    nxt = lax.rem(u + 1, n_user)
    prv = lax.rem(u + n_user - 1, n_user)
    home = lax.rem(u + n_user - (VISITS - 1), n_user)
    guest = lax.rem(u + VISITS - 1, n_user)

    load_p = pltpu.make_async_copy(p_hbm, p_v, load_sem.at[0])
    load_q = pltpu.make_async_copy(q_hbm, q_in.at[0], load_sem.at[1])
    load_c = pltpu.make_async_copy(c_hbm, c_v, load_sem.at[2])
    load_p.start()
    load_q.start()
    load_c.start()

    barrier = pltpu.get_barrier_semaphore()
    for other in (nxt, prv, home, guest):
        pl.semaphore_signal(
            barrier, inc=1, device_id={"user": other}, device_id_type=MESH
        )

    @pl.when((core == 0) & (s > 0))
    def _():
        pl.semaphore_signal(
            barrier, inc=1, device_id={"isec": s - 1}, device_id_type=MESH
        )

    @pl.when((core == 0) & (s < last))
    def _():
        pl.semaphore_signal(
            barrier, inc=1, device_id={"isec": s + 1}, device_id_type=MESH
        )

    load_p.wait()
    for i in range(user_tiles):
        rows = pl.ds(i * TILE, TILE)
        high, low = halves(p_v[rows, :])
        p_hi[rows, :] = high
        p_lo[rows, :] = low
    load_q.wait()
    load_c.wait()

    def errors(visit):
        high, low = halves(q_in[visit])
        q_hi[...] = high
        q_lo[...] = low
        for i in range(user_tiles):
            rows = pl.ds(i * TILE, TILE)
            x = dot3(
                (p_hi[rows, :], p_lo[rows, :]), (q_hi[...], q_lo[...]), ((1,), (1,))
            )
            for j in range(item_tiles):
                k = i * item_tiles + j
                place = jnp.int32(0)
                live = jnp.int32(0)
                for n in range(c_v.shape[1]):
                    hit = (ids_ref[visit, n] == k) & (n < counts_ref[visit])
                    place = place + jnp.where(hit, n, 0)
                    live = live + jnp.where(hit, 1, 0)
                columns = slice(j * TILE, (j + 1) * TILE)
                weight = c_v[visit, place].astype(F32)
                e = jnp.where(live > 0, weight * (x[:, columns] - 1.0), 0.0)
                high, low = halves(e)
                e_hi[rows, pl.ds(j * TILE, TILE)] = high
                e_lo[rows, pl.ds(j * TILE, TILE)] = low
                high, low = halves(e.T)
                et_hi[pl.ds(j * TILE, TILE), rows] = high
                et_lo[pl.ds(j * TILE, TILE), rows] = low

    def item_step(visit):
        for j in range(item_tiles):
            rows = pl.ds(j * TILE, TILE)
            d = dot3(
                (et_hi[rows, :], et_lo[rows, :]), (p_hi[...], p_lo[...]), ((1,), (0,))
            )
            q = q_in[visit, rows, :]
            q_out[visit, rows, :] = q - item_rate * (d + shrinkage * q)

    def user_step(visit):
        for i in range(user_tiles):
            rows = pl.ds(i * TILE, TILE)
            g = dot3(
                (e_hi[rows, :], e_lo[rows, :]), (q_hi[...], q_lo[...]), ((1,), (0,))
            )
            if visit == 0:
                g_v[rows, :] = g
            else:
                g_v[rows, :] = g_v[rows, :] + g

    def moved(visit):
        if visit < VISITS - 1:
            target, place = nxt, q_in.at[visit + 1]
        else:
            target, place = home, items_ref
        return pltpu.make_async_remote_copy(
            src_ref=q_out.at[visit],
            dst_ref=place,
            send_sem=send_sem.at[visit],
            recv_sem=recv_sem.at[visit],
            device_id={"user": target},
            device_id_type=MESH,
        )

    def gradient_over(other):
        return pltpu.make_async_remote_copy(
            src_ref=g_v,
            dst_ref=g_peer,
            send_sem=g_send,
            recv_sem=g_recv,
            device_id={"user": other},
            device_id_type=MESH,
        )

    def run_copy(who, way, d, source, target):
        return pltpu.make_async_remote_copy(
            src_ref=source,
            dst_ref=runs.at[who, way, d],
            send_sem=run_send.at[who, way, d],
            recv_sem=run_recv.at[who, way, d],
            device_id={"isec": target},
            device_id_type=MESH,
        )

    def shard(ref, d):
        return ref.at[pl.ds(pl.multiple_of(d * share, share), share), :]

    def reduce_line(who, g_ref):
        def step(t, carry):
            d = last + s - t

            @pl.when(t >= s)
            def _():
                @pl.when(s > 0)
                def _():
                    run_copy(who, 0, d, runs.at[who, 0, d], s).wait_recv()

                @pl.when((d > s) & (s > 0))
                def _():
                    runs[who, 0, d] = runs[who, 0, d] + shard(g_ref, d)[...]
                    run_copy(who, 0, d, runs.at[who, 0, d], s + 1).start()

                @pl.when((d > s) & (s == 0))
                def _():
                    run_copy(who, 0, d, shard(g_ref, d), s + 1).start()

            b = t - last + s

            @pl.when(t >= last - s)
            def _():
                @pl.when(s < last)
                def _():
                    run_copy(who, 1, b, runs.at[who, 1, b], s).wait_recv()

                @pl.when((b < s) & (s < last))
                def _():
                    runs[who, 1, b] = runs[who, 1, b] + shard(g_ref, b)[...]
                    run_copy(who, 1, b, runs.at[who, 1, b], s - 1).start()

                @pl.when((b < s) & (s == last))
                def _():
                    run_copy(who, 1, b, shard(g_ref, b), s - 1).start()

            return carry

        lax.fori_loop(0, n_isec, step, 0)

    def line_total(who, g_ref):
        mine = shard(g_ref, s)[...]
        right = jnp.where(s > 0, runs[who, 0, s], 0.0)
        left = jnp.where(s < last, runs[who, 1, s], 0.0)
        return mine + (right + left)

    def drain_line(who, g_ref):
        def step(d, carry):
            @pl.when(d > s)
            def _():
                run_copy(who, 0, d, runs.at[who, 0, d], s).wait_send()

            @pl.when(d < s)
            def _():
                run_copy(who, 1, d, runs.at[who, 1, d], s).wait_send()

            return carry

        lax.fori_loop(0, n_isec, step, 0)

    def finish(total):
        own = p_v[pl.ds(pl.multiple_of(s * share, share), share), :]
        users_ref[...] = own - user_rate * (total + shrinkage * own)

    def finish_copy(other):
        return pltpu.make_async_remote_copy(
            src_ref=fin_out,
            dst_ref=fin_in,
            send_sem=fin_send,
            recv_sem=fin_recv,
            device_id={"user": other},
            device_id_type=MESH,
        )

    for visit in range(VISITS):
        if visit > 0:
            moved(visit - 1).wait_recv()
        errors(visit)
        if visit == 0:
            item_step(visit)
            greeted = jnp.where(s > 0, 1, 0) + jnp.where(s < last, 1, 0)
            pl.semaphore_wait(barrier, 4 + jnp.where(core == 0, greeted, 0))
            moved(visit).start()
            user_step(visit)
        elif visit < VISITS - 1:
            item_step(visit)
            moved(visit).start()
            user_step(visit)
        else:
            user_step(visit)

            @pl.when(core == 1)
            def _():
                gradient_over(prv).start()

            item_step(visit)
            moved(visit).start()

        if visit == VISITS - 2:

            @pl.when(core == 0)
            def _():
                gradient_over(prv).wait_recv()
                reduce_line(0, g_peer)
                fin_out[...] = line_total(0, g_peer)
                finish_copy(nxt).start()

    @pl.when(core == 0)
    def _():
        reduce_line(1, g_v)
        finish(line_total(1, g_v))
        drain_line(0, g_peer)
        drain_line(1, g_v)
        finish_copy(nxt).wait_send()

    @pl.when(core == 1)
    def _():
        gradient_over(prv).wait_send()
        finish_copy(nxt).wait_recv()
        finish(fin_in[...])

    for visit in range(VISITS):
        moved(visit).wait_send()
    moved(VISITS - 1).wait_recv()


def on_device(n_user, n_isec, user_factors, item_factors, confidence, tile_ids, tile_counts):
    user_rows, rank = user_factors.shape
    block = item_factors.shape[0]
    tiles = confidence.shape[3]
    share = user_rows // n_isec
    vmem = functools.partial(pltpu.VMEM, dtype=F32)
    dma = pltpu.SemaphoreType.DMA
    return pl.pallas_call(
        functools.partial(kernel, n_user, n_isec),
        out_shape=(
            jax.ShapeDtypeStruct((share, rank), F32),
            jax.ShapeDtypeStruct((block, rank), F32),
        ),
        in_specs=[pl.BlockSpec(memory_space=pltpu.SMEM)] * 2
        + [pl.BlockSpec(memory_space=pl.ANY)] * 3,
        out_specs=(
            pl.BlockSpec(memory_space=pltpu.VMEM),
            pl.BlockSpec(memory_space=pl.ANY),
        ),
        scratch_shapes=[
            vmem((user_rows, rank)),
            pltpu.VMEM((user_rows, rank), BF16),
            pltpu.VMEM((user_rows, rank), BF16),
            vmem((VISITS, block, rank)),
            vmem((VISITS, block, rank)),
            pltpu.VMEM((block, rank), BF16),
            pltpu.VMEM((block, rank), BF16),
            pltpu.VMEM((VISITS, tiles, TILE, TILE), BF16),
            pltpu.VMEM((block, user_rows), BF16),
            pltpu.VMEM((block, user_rows), BF16),
            pltpu.VMEM((user_rows, block), BF16),
            pltpu.VMEM((user_rows, block), BF16),
            vmem((user_rows, rank)),
            vmem((user_rows, rank)),
            vmem((2, 2, n_isec, share, rank)),
            vmem((share, rank)),
            vmem((share, rank)),
            dma((3,)),
            dma((VISITS,)),
            dma((VISITS,)),
            dma,
            dma,
            dma((2, 2, n_isec)),
            dma((2, 2, n_isec)),
            dma,
            dma,
        ],
        compiler_params=pltpu.CompilerParams(
            collective_id=0, has_side_effects=True
        ),
        name="window",
    )(tile_ids[0, 0], tile_counts[0, 0], user_factors, item_factors, confidence[0, 0])


def solution(mesh):
    sizes = dict(mesh.shape)
    return jax.shard_map(
        functools.partial(on_device, sizes["user"], sizes["isec"]),
        mesh=mesh,
        in_specs=(
            P("user", None),
            P(("user", "isec"), None),
            P("user", "isec", None, None, None, None),
            P("user", "isec", None, None),
            P("user", "isec", None),
        ),
        out_specs=(P(("user", "isec"), None), P(("user", "isec"), None)),
        check_vma=False,
    )
```

```python
import functools

import jax
import jax.numpy as jnp
from jax import lax
from jax.experimental import pallas as pl
from jax.experimental.pallas import tpu as pltpu
from jax.sharding import PartitionSpec as P

TILE = 128
VISITS = 4
CHUNKS = 4
PARTS = 2
LEAD = 3

item_rate = 0.02
user_rate = 0.005
shrinkage = 0.1

MESH = pl.DeviceIdType.MESH
F32 = jnp.float32
BF16 = jnp.bfloat16


def halves(value):
    high = value.astype(BF16)
    low = (value - high.astype(F32)).astype(BF16)
    return high, low


def dot3(left, right, dims):
    one = functools.partial(
        lax.dot_general, dimension_numbers=(dims, ((), ())), preferred_element_type=F32
    )
    return one(left[0], right[0]) + (one(left[0], right[1]) + one(left[1], right[0]))


def kernel(
    n_user, n_isec,
    ids_ref, counts_ref, p_hbm, q_hbm, c_hbm,
    users_ref, items_ref,
    p_v, p_hi, p_lo, q_in, q_out, q_hi, q_lo, c_v, et_hi, et_lo, e_hi, e_lo,
    g_v, g_peer, runs, fin_out, fin_in, relay,
    load_sem, near_send, near_recv, far_send, hop_recv, far_recv,
    g_send, g_recv, run_send, run_recv, fin_send, fin_recv,
):
    user_rows, rank = p_v.shape
    block = q_in.shape[1]
    user_tiles = user_rows // TILE
    item_tiles = block // TILE
    share = user_rows // n_isec
    last = n_isec - 1

    ring = 2 * n_isec
    chunks = hop_recv.shape[3]
    chunk_rows = block // 2 // chunks

    u = lax.axis_index("user")
    s = lax.axis_index("isec")
    core = lax.rem(u, 2)
    column = u // 4
    z = lax.rem(u // 2, 2) * n_isec + s
    nxt = lax.rem(u + 1, n_user)
    prv = lax.rem(u + n_user - 1, n_user)
    home = lax.rem(u + n_user - (VISITS - 1), n_user)
    guest = lax.rem(u + VISITS - 1, n_user)
    way_step = (1, ring - 1)

    def owner(col, z_at, at_core):
        return (col * 2 + z_at // n_isec) * 2 + at_core

    def chip(col, z_at, at_core):
        z_at = lax.rem(z_at, ring)
        return {"user": owner(col, z_at, at_core), "isec": lax.rem(z_at, n_isec)}

    def shift_of(visit):
        return 1 if visit < VISITS - 1 else n_user - (VISITS - 1)

    def relay_target(way, visit):
        source = lax.rem(z + (ring - way_step[way]) * (n_isec - 1), ring)
        first = owner(column, source, 1)
        return {
            "user": lax.rem(first + shift_of(visit), n_user),
            "isec": lax.rem(source, n_isec),
        }

    def relay_origin(way, visit):
        first = lax.rem(u + n_user - shift_of(visit), n_user)
        return chip(first // 4, z + ring - way_step[way], 1)

    load_q = pltpu.make_async_copy(q_hbm, q_in.at[0], load_sem.at[user_tiles])
    load_c = pltpu.make_async_copy(c_hbm, c_v, load_sem.at[user_tiles + 1])

    def load_p(i):
        rows = pl.ds(i * TILE, TILE)
        return pltpu.make_async_copy(p_hbm.at[rows, :], p_v.at[rows, :], load_sem.at[i])

    for i in range(user_tiles):
        load_p(i).start()
    load_q.start()
    load_c.start()

    barrier = pltpu.get_barrier_semaphore()

    def greet(device):
        pl.semaphore_signal(barrier, inc=1, device_id=device, device_id_type=MESH)

    @pl.when(core == 1)
    def _():
        for way in range(2):
            greet(chip(column, z + way_step[way], 1))
            greet(relay_target(way, 0))
            greet(relay_target(way, VISITS - 1))
        greet({"user": prv})
        greet({"user": guest})

    @pl.when(core == 0)
    def _():
        for way in range(2):
            greet(relay_origin(way, 0))
            greet(relay_origin(way, VISITS - 1))
        greet({"user": nxt})
        greet({"user": home})

    @pl.when((core == 0) & (s > 0))
    def _():
        greet({"isec": s - 1})

    @pl.when((core == 0) & (s < last))
    def _():
        greet({"isec": s + 1})

    for i in range(user_tiles):
        load_p(i).wait()
        rows = pl.ds(i * TILE, TILE)
        high, low = halves(p_v[rows, :])
        p_hi[rows, :] = high
        p_lo[rows, :] = low
    load_q.wait()
    load_c.wait()

    def errors(visit):
        high, low = halves(q_in[visit])
        q_hi[...] = high
        q_lo[...] = low
        for i in range(user_tiles):
            rows = pl.ds(i * TILE, TILE)
            x = dot3(
                (p_hi[rows, :], p_lo[rows, :]), (q_hi[...], q_lo[...]), ((1,), (1,))
            )
            for j in range(item_tiles):
                k = i * item_tiles + j
                place = jnp.int32(0)
                live = jnp.int32(0)
                for n in range(c_v.shape[1]):
                    hit = (ids_ref[visit, n] == k) & (n < counts_ref[visit])
                    place = place + jnp.where(hit, n, 0)
                    live = live + jnp.where(hit, 1, 0)
                columns = slice(j * TILE, (j + 1) * TILE)
                weight = c_v[visit, place].astype(F32)
                e = jnp.where(live > 0, weight * (x[:, columns] - 1.0), 0.0)
                high, low = halves(e)
                e_hi[rows, pl.ds(j * TILE, TILE)] = high
                e_lo[rows, pl.ds(j * TILE, TILE)] = low
                high, low = halves(e.T)
                et_hi[pl.ds(j * TILE, TILE), rows] = high
                et_lo[pl.ds(j * TILE, TILE), rows] = low

    def item_step(visit):
        for j in range(item_tiles):
            rows = pl.ds(j * TILE, TILE)
            d = dot3(
                (et_hi[rows, :], et_lo[rows, :]), (p_hi[...], p_lo[...]), ((1,), (0,))
            )
            q = q_in[visit, rows, :]
            q_out[visit, rows, :] = q - item_rate * (d + shrinkage * q)

    def user_step(visit):
        for i in range(user_tiles):
            rows = pl.ds(i * TILE, TILE)
            g = dot3(
                (e_hi[rows, :], e_lo[rows, :]), (q_hi[...], q_lo[...]), ((1,), (0,))
            )
            if visit == 0:
                g_v[rows, :] = g
            else:
                g_v[rows, :] = g_v[rows, :] + g

    def near(visit):
        return pltpu.make_async_remote_copy(
            src_ref=q_out.at[visit],
            dst_ref=q_in.at[visit + 1] if visit < VISITS - 1 else items_ref,
            send_sem=near_send.at[visit],
            recv_sem=near_recv.at[visit],
            device_id={"user": nxt if visit < VISITS - 1 else home},
            device_id_type=MESH,
        )

    def piece(way, part):
        return pl.ds(way * chunks * chunk_rows + part * chunk_rows, chunk_rows)

    def hop(visit, way, index, part, arrived=False):
        rows = pl.ds(part * chunk_rows, chunk_rows)
        if arrived:
            source = relay.at[visit, way, index, rows, :]
        elif isinstance(index, int) and index == 0:
            source = q_out.at[visit, piece(way, part), :]
        else:
            source = relay.at[visit, way, index - 1, rows, :]
        return pltpu.make_async_remote_copy(
            src_ref=source,
            dst_ref=relay.at[visit, way, index, rows, :],
            send_sem=far_send.at[visit, way],
            recv_sem=hop_recv.at[visit, way, index, part],
            device_id=chip(column, z + way_step[way], 1),
            device_id_type=MESH,
        )

    def final_hop(visit, way, part):
        rows = pl.ds(part * chunk_rows, chunk_rows)
        landing = q_in.at[visit + 1] if visit < VISITS - 1 else items_ref
        return pltpu.make_async_remote_copy(
            src_ref=relay.at[visit, way, n_isec - 2, rows, :],
            dst_ref=landing.at[piece(way, part), :],
            send_sem=far_send.at[visit, way],
            recv_sem=far_recv.at[visit],
            device_id=relay_target(way, visit),
            device_id_type=MESH,
        )

    def depart(visit):
        for part in range(chunks):
            for way in range(2):
                hop(visit, way, 0, part).start()

    def pass_on(visit, first, end):
        def step(index, carry):
            for part in range(chunks):
                for way in range(2):
                    hop(visit, way, index, part, True).wait_recv()
                    hop(visit, way, index + 1, part).start()
            return carry

        lax.fori_loop(first, end, step, 0)

    def arrive(visit):
        for part in range(chunks):
            for way in range(2):
                hop(visit, way, n_isec - 2, part, True).wait_recv()
                final_hop(visit, way, part).start()

    def whole(source, landing, visit, way):
        return pltpu.make_async_remote_copy(
            src_ref=source,
            dst_ref=landing,
            send_sem=far_send.at[visit, way],
            recv_sem=far_recv.at[visit],
            device_id=chip(column, z + 1, 1),
            device_id_type=MESH,
        )

    def landed(visit):
        landing = q_in.at[visit + 1] if visit < VISITS - 1 else items_ref
        whole(q_out.at[visit], landing, visit, 0).wait_recv()

    def drain_far():
        for visit in range(VISITS):
            for way in range(2):
                hops = relay.at[visit, way]
                whole(hops, hops, visit, way).wait_send()

    def gradient_over(other):
        return pltpu.make_async_remote_copy(
            src_ref=g_v,
            dst_ref=g_peer,
            send_sem=g_send,
            recv_sem=g_recv,
            device_id={"user": other},
            device_id_type=MESH,
        )

    parts = runs.shape[3]
    part_rows = share // parts

    def run_copy(who, way, d, part, source, target):
        return pltpu.make_async_remote_copy(
            src_ref=source,
            dst_ref=runs.at[who, way, d, part],
            send_sem=run_send.at[who],
            recv_sem=run_recv.at[who, way, d, part],
            device_id={"isec": target},
            device_id_type=MESH,
        )

    def shard(ref, d, part):
        start = pl.multiple_of(d * share + part * part_rows, part_rows)
        return ref.at[pl.ds(start, part_rows), :]

    def run_step(who, g_ref, way, d, target, inner, outer, sends):
        @pl.when(inner)
        def _():
            for part in range(parts):
                run = runs.at[who, way, d, part]
                run_copy(who, way, d, part, run, s).wait_recv()

                @pl.when(sends)
                def _():
                    run[...] = run[...] + shard(g_ref, d, part)[...]
                    run_copy(who, way, d, part, run, target).start()

        @pl.when(outer & sends)
        def _():
            for part in range(parts):
                run_copy(who, way, d, part, shard(g_ref, d, part), target).start()

    def line_step(who, g_ref, t):
        d = last + s - t

        @pl.when(t >= s)
        def _():
            run_step(who, g_ref, 0, d, s + 1, s > 0, s == 0, d > s)

        b = t - last + s

        @pl.when(t >= last - s)
        def _():
            run_step(who, g_ref, 1, b, s - 1, s < last, s == last, b < s)

    def line_total(who, g_ref, part):
        mine = shard(g_ref, s, part)[...]
        right = jnp.where(s > 0, runs[who, 0, s, part], 0.0)
        left = jnp.where(s < last, runs[who, 1, s, part], 0.0)
        return mine + (right + left)

    def drain_line(who, g_ref):
        sent = g_ref.at[pl.ds(0, last * share), :]
        pltpu.make_async_remote_copy(
            src_ref=sent,
            dst_ref=sent,
            send_sem=run_send.at[who],
            recv_sem=fin_recv,
            device_id={"isec": lax.rem(s + 1, n_isec)},
            device_id_type=MESH,
        ).wait_send()

    def finish(total, part):
        own = shard(p_v, s, part)[...]
        rows = pl.ds(part * part_rows, part_rows)
        users_ref[rows, :] = own - user_rate * (total + shrinkage * own)

    def finish_copy(other):
        return pltpu.make_async_remote_copy(
            src_ref=fin_out,
            dst_ref=fin_in,
            send_sem=fin_send,
            recv_sem=fin_recv,
            device_id={"user": other},
            device_id_type=MESH,
        )

    errors(0)
    item_step(0)

    @pl.when(core == 0)
    def _():
        greeted = jnp.where(s > 0, 1, 0) + jnp.where(s < last, 1, 0)
        pl.semaphore_wait(barrier, 6 + greeted)
        near(0).start()
        user_step(0)
        for visit in range(1, VISITS - 1):
            landed(visit - 1)
            errors(visit)
            item_step(visit)
            near(visit).start()
            user_step(visit)
        gradient_over(prv).wait_recv()

        def first_steps(t, carry):
            line_step(0, g_peer, t)
            return carry

        def both_steps(t, carry):
            line_step(0, g_peer, t)
            line_step(1, g_v, t - LEAD)
            return carry

        def last_steps(t, carry):
            line_step(1, g_v, t)
            return carry

        lax.fori_loop(0, LEAD, first_steps, 0)
        landed(VISITS - 2)
        errors(VISITS - 1)
        user_step(VISITS - 1)
        item_step(VISITS - 1)
        near(VISITS - 1).start()
        lax.fori_loop(LEAD, n_isec, both_steps, 0)
        for part in range(parts):
            rows = pl.ds(part * part_rows, part_rows)
            fin_out[rows, :] = line_total(0, g_peer, part)
        finish_copy(nxt).start()
        lax.fori_loop(n_isec - LEAD, n_isec, last_steps, 0)
        for part in range(parts):
            finish(line_total(1, g_v, part), part)
        drain_line(0, g_peer)
        drain_line(1, g_v)
        finish_copy(nxt).wait_send()
        for visit in range(VISITS):
            near(visit).wait_send()
        landed(VISITS - 1)

    @pl.when(core == 1)
    def _():
        pl.semaphore_wait(barrier, 8)
        depart(0)
        user_step(0)
        near(0).wait_recv()
        errors(1)
        item_step(1)
        user_step(1)
        pass_on(0, 0, n_isec - 2)
        arrive(0)
        depart(1)
        pass_on(1, 0, 3)
        near(1).wait_recv()
        errors(2)
        pass_on(1, 3, 4)
        item_step(2)
        pass_on(1, 4, 5)
        user_step(2)
        pass_on(1, 5, n_isec - 2)
        arrive(1)
        depart(2)
        pass_on(2, 0, 2)
        near(2).wait_recv()
        errors(3)
        pass_on(2, 2, 3)
        user_step(3)
        gradient_over(prv).start()
        item_step(3)
        pass_on(2, 3, n_isec - 2)
        arrive(2)
        depart(3)
        pass_on(3, 0, n_isec - 2)
        arrive(3)
        gradient_over(prv).wait_send()
        finish_copy(nxt).wait_recv()
        for part in range(parts):
            finish(fin_in[pl.ds(part * part_rows, part_rows), :], part)
        drain_far()
        near(VISITS - 1).wait_recv()


def settle_kernel(users_ref, items_ref, users_out, items_out, users_v, items_v, sem_in, sem_out):
    count = sem_in.shape[0] - 1
    rows = items_v.shape[0] // count

    def moves(users_from, users_to, items_from, items_to, sem):
        yield pltpu.make_async_copy(users_from, users_to, sem.at[count])
        for i in range(count):
            at = pl.ds(i * rows, rows)
            yield pltpu.make_async_copy(items_from.at[at, :], items_to.at[at, :], sem.at[i])

    into = list(moves(users_ref, users_v, items_ref, items_v, sem_in))
    out = list(moves(users_v, users_out, items_v, items_out, sem_out))
    for copy in into:
        copy.start()
    for first, second in zip(into, out):
        first.wait()
        second.start()
    for copy in out:
        copy.wait()


def settle(users, items):
    return pl.pallas_call(
        settle_kernel,
        out_shape=(
            jax.ShapeDtypeStruct(users.shape, F32),
            jax.ShapeDtypeStruct(items.shape, F32),
        ),
        in_specs=[pl.BlockSpec(memory_space=pl.ANY)] * 2,
        out_specs=(pl.BlockSpec(memory_space=pl.ANY),) * 2,
        scratch_shapes=[
            pltpu.VMEM(users.shape, F32),
            pltpu.VMEM(items.shape, F32),
            pltpu.SemaphoreType.DMA((5,)),
            pltpu.SemaphoreType.DMA((5,)),
        ],
        name="settle",
    )(users, items)


def on_device(n_user, n_isec, user_factors, item_factors, confidence, tile_ids, tile_counts):
    user_rows, rank = user_factors.shape
    block = item_factors.shape[0]
    tiles = confidence.shape[3]
    share = user_rows // n_isec
    vmem = functools.partial(pltpu.VMEM, dtype=F32)
    dma = pltpu.SemaphoreType.DMA
    users, items = pl.pallas_call(
        functools.partial(kernel, n_user, n_isec),
        out_shape=(
            jax.ShapeDtypeStruct((share, rank), F32),
            jax.ShapeDtypeStruct((block, rank), F32),
        ),
        in_specs=[pl.BlockSpec(memory_space=pltpu.SMEM)] * 2
        + [pl.BlockSpec(memory_space=pl.ANY)] * 3,
        out_specs=(
            pl.BlockSpec(memory_space=pltpu.VMEM),
            pl.BlockSpec(memory_space=pl.ANY),
        ),
        scratch_shapes=[
            vmem((user_rows, rank)),
            pltpu.VMEM((user_rows, rank), BF16),
            pltpu.VMEM((user_rows, rank), BF16),
            vmem((VISITS, block, rank)),
            vmem((VISITS, block, rank)),
            pltpu.VMEM((block, rank), BF16),
            pltpu.VMEM((block, rank), BF16),
            pltpu.VMEM((VISITS, tiles, TILE, TILE), BF16),
            pltpu.VMEM((block, user_rows), BF16),
            pltpu.VMEM((block, user_rows), BF16),
            pltpu.VMEM((user_rows, block), BF16),
            pltpu.VMEM((user_rows, block), BF16),
            vmem((user_rows, rank)),
            vmem((user_rows, rank)),
            vmem((2, 2, n_isec, PARTS, share // PARTS, rank)),
            vmem((share, rank)),
            vmem((share, rank)),
            vmem((VISITS, 2, n_isec, block // 2, rank)),
            dma((user_rows // TILE + 2,)),
            dma((VISITS,)),
            dma((VISITS,)),
            dma((VISITS, 2)),
            dma((VISITS, 2, n_isec - 1, CHUNKS)),
            dma((VISITS,)),
            dma,
            dma,
            dma((2,)),
            dma((2, 2, n_isec, PARTS)),
            dma,
            dma,
        ],
        compiler_params=pltpu.CompilerParams(
            collective_id=0, has_side_effects=True
        ),
        name="window",
    )(tile_ids[0, 0], tile_counts[0, 0], user_factors, item_factors, confidence[0, 0])
    return settle(users, items)


def solution(mesh):
    sizes = dict(mesh.shape)
    return jax.shard_map(
        functools.partial(on_device, sizes["user"], sizes["isec"]),
        mesh=mesh,
        in_specs=(
            P("user", None),
            P(("user", "isec"), None),
            P("user", "isec", None, None, None, None),
            P("user", "isec", None, None),
            P("user", "isec", None),
        ),
        out_specs=(P(("user", "isec"), None), P(("user", "isec"), None)),
        check_vma=False,
    )
```

```python
import functools

import jax
import jax.numpy as jnp
from jax import lax
from jax.experimental import pallas as pl
from jax.experimental.pallas import tpu as pltpu
from jax.sharding import PartitionSpec as P

TILE = 128
VISITS = 4
CHUNKS = 4
PARTS = 2
LEAD = 4
PACE = (2, 2)
STARTS = 2
STRIDE = 1

item_rate = 0.02
user_rate = 0.005
shrinkage = 0.1

MESH = pl.DeviceIdType.MESH
F32 = jnp.float32
BF16 = jnp.bfloat16


def halves(value):
    high = value.astype(BF16)
    low = (value - high.astype(F32)).astype(BF16)
    return high, low


def dot3(left, right, dims):
    one = functools.partial(
        lax.dot_general, dimension_numbers=(dims, ((), ())), preferred_element_type=F32
    )
    return one(left[0], right[0]) + (one(left[0], right[1]) + one(left[1], right[0]))


def kernel(
    n_user, n_isec,
    ids_hbm, counts_hbm, p_hbm, q_hbm, c_hbm,
    users_ref, items_ref,
    ids_ref, counts_ref,
    p_v, p_hi, p_lo, q_in, q_out, q_hi, q_lo, c_v, et_hi, et_lo, e_hi, e_lo,
    g_v, g_peer, runs, fin_out, fin_in, relay,
    load_sem, near_send, near_recv, far_send, hop_recv, far_recv,
    g_send, g_recv, run_send, run_recv, fin_send, fin_recv,
):
    user_rows, rank = p_v.shape
    block = q_in.shape[1]
    user_tiles = user_rows // TILE
    item_tiles = block // TILE
    share = user_rows // n_isec
    last = n_isec - 1

    ring = 2 * n_isec
    chunks = hop_recv.shape[3]
    hops = hop_recv.shape[2] + 1
    stride = n_isec // hops
    chunk_rows = block // 2 // chunks

    u = lax.axis_index("user")
    s = lax.axis_index("isec")
    core = lax.rem(u, 2)
    column = u // 4
    z = lax.rem(u // 2, 2) * n_isec + s
    nxt = lax.rem(u + 1, n_user)
    prv = lax.rem(u + n_user - 1, n_user)
    home = lax.rem(u + n_user - (VISITS - 1), n_user)
    guest = lax.rem(u + VISITS - 1, n_user)
    way_step = (stride, ring - stride)

    def owner(col, z_at, at_core):
        return (col * 2 + z_at // n_isec) * 2 + at_core

    def chip(col, z_at, at_core):
        z_at = lax.rem(z_at, ring)
        return {"user": owner(col, z_at, at_core), "isec": lax.rem(z_at, n_isec)}

    def shift_of(visit):
        return 1 if visit < VISITS - 1 else n_user - (VISITS - 1)

    def relay_target(way, visit):
        source = lax.rem(z + (ring - way_step[way]) * (hops - 1), ring)
        first = owner(column, source, 1)
        return {
            "user": lax.rem(first + shift_of(visit), n_user),
            "isec": lax.rem(source, n_isec),
        }

    def relay_origin(way, visit):
        first = lax.rem(u + n_user - shift_of(visit), n_user)
        return chip(first // 4, z + ring - way_step[way], 1)

    load_q = pltpu.make_async_copy(q_hbm, q_in.at[0], load_sem.at[user_tiles])
    load_c = pltpu.make_async_copy(c_hbm, c_v, load_sem.at[user_tiles + 1])

    def load_p(i):
        rows = pl.ds(i * TILE, TILE)
        return pltpu.make_async_copy(p_hbm.at[rows, :], p_v.at[rows, :], load_sem.at[i])

    load_ids = pltpu.make_async_copy(ids_hbm, ids_ref, load_sem.at[user_tiles + 2])
    load_counts = pltpu.make_async_copy(
        counts_hbm, counts_ref, load_sem.at[user_tiles + 3]
    )

    for i in range(user_tiles):
        load_p(i).start()
    load_ids.start()
    load_counts.start()
    load_q.start()
    load_c.start()

    barrier = pltpu.get_barrier_semaphore()

    def greet(device):
        pl.semaphore_signal(barrier, inc=1, device_id=device, device_id_type=MESH)

    @pl.when(core == 1)
    def _():
        for way in range(2):
            greet(chip(column, z + way_step[way], 1))
            greet(relay_target(way, 0))
            greet(relay_target(way, VISITS - 1))
        greet({"user": prv})
        greet({"user": guest})

    @pl.when(core == 0)
    def _():
        for way in range(2):
            greet(relay_origin(way, 0))
            greet(relay_origin(way, VISITS - 1))
        greet({"user": nxt})
        greet({"user": home})

    @pl.when((core == 0) & (s > 0))
    def _():
        greet({"isec": s - 1})

    @pl.when((core == 0) & (s < last))
    def _():
        greet({"isec": s + 1})

    for i in range(user_tiles):
        load_p(i).wait()
        rows = pl.ds(i * TILE, TILE)
        high, low = halves(p_v[rows, :])
        p_hi[rows, :] = high
        p_lo[rows, :] = low
    load_q.wait()
    load_c.wait()
    load_ids.wait()
    load_counts.wait()

    def split_items(visit):
        high, low = halves(q_in[visit])
        q_hi[...] = high
        q_lo[...] = low

    def errors_of(visit, i):
        rows = pl.ds(i * TILE, TILE)
        x = dot3((p_hi[rows, :], p_lo[rows, :]), (q_hi[...], q_lo[...]), ((1,), (1,)))
        for j in range(item_tiles):
            k = i * item_tiles + j
            place = jnp.int32(0)
            live = jnp.int32(0)
            for n in range(c_v.shape[1]):
                hit = (ids_ref[visit, n] == k) & (n < counts_ref[visit])
                place = place + jnp.where(hit, n, 0)
                live = live + jnp.where(hit, 1, 0)
            columns = slice(j * TILE, (j + 1) * TILE)
            weight = c_v[visit, place].astype(F32)
            e = jnp.where(live > 0, weight * (x[:, columns] - 1.0), 0.0)
            high, low = halves(e)
            e_hi[rows, pl.ds(j * TILE, TILE)] = high
            e_lo[rows, pl.ds(j * TILE, TILE)] = low
            high, low = halves(e.T)
            et_hi[pl.ds(j * TILE, TILE), rows] = high
            et_lo[pl.ds(j * TILE, TILE), rows] = low

    def item_step_of(visit, j):
        rows = pl.ds(j * TILE, TILE)
        d = dot3(
            (et_hi[rows, :], et_lo[rows, :]), (p_hi[...], p_lo[...]), ((1,), (0,))
        )
        q = q_in[visit, rows, :]
        q_out[visit, rows, :] = q - item_rate * (d + shrinkage * q)

    def user_step_of(visit, i):
        rows = pl.ds(i * TILE, TILE)
        g = dot3(
            (e_hi[rows, :], e_lo[rows, :]), (q_hi[...], q_lo[...]), ((1,), (0,))
        )
        if visit == 0:
            g_v[rows, :] = g
        else:
            g_v[rows, :] = g_v[rows, :] + g

    def errors(visit):
        split_items(visit)
        for i in range(user_tiles):
            errors_of(visit, i)

    def item_step(visit):
        for j in range(item_tiles):
            item_step_of(visit, j)

    def user_step(visit):
        for i in range(user_tiles):
            user_step_of(visit, i)

    def pieces(visit):
        work = [lambda: near(visit - 1).wait_recv(), lambda: split_items(visit)]
        work += [functools.partial(errors_of, visit, i) for i in range(user_tiles)]
        users_part = [functools.partial(user_step_of, visit, i) for i in range(user_tiles)]
        items_part = [functools.partial(item_step_of, visit, j) for j in range(item_tiles)]
        if visit < VISITS - 1:
            return work + items_part + users_part
        return work + users_part + [lambda: gradient_over(prv).start()] + items_part

    def near(visit):
        return pltpu.make_async_remote_copy(
            src_ref=q_out.at[visit],
            dst_ref=q_in.at[visit + 1] if visit < VISITS - 1 else items_ref,
            send_sem=near_send.at[visit],
            recv_sem=near_recv.at[visit],
            device_id={"user": nxt if visit < VISITS - 1 else home},
            device_id_type=MESH,
        )

    def piece(way, part):
        return pl.ds(way * chunks * chunk_rows + part * chunk_rows, chunk_rows)

    def hop(visit, way, index, part, arrived=False):
        rows = pl.ds(part * chunk_rows, chunk_rows)
        if arrived:
            source = relay.at[visit, way, index, rows, :]
        elif isinstance(index, int) and index == 0:
            source = q_out.at[visit, piece(way, part), :]
        else:
            source = relay.at[visit, way, index - 1, rows, :]
        return pltpu.make_async_remote_copy(
            src_ref=source,
            dst_ref=relay.at[visit, way, index, rows, :],
            send_sem=far_send.at[visit, way],
            recv_sem=hop_recv.at[visit, way, index, part],
            device_id=chip(column, z + way_step[way], 1),
            device_id_type=MESH,
        )

    def final_hop(visit, way, part):
        rows = pl.ds(part * chunk_rows, chunk_rows)
        landing = q_in.at[visit + 1] if visit < VISITS - 1 else items_ref
        return pltpu.make_async_remote_copy(
            src_ref=relay.at[visit, way, hops - 2, rows, :],
            dst_ref=landing.at[piece(way, part), :],
            send_sem=far_send.at[visit, way],
            recv_sem=far_recv.at[visit],
            device_id=relay_target(way, visit),
            device_id_type=MESH,
        )

    def depart(visit):
        for part in range(chunks):
            for way in range(2):
                hop(visit, way, 0, part).start()

    def relay_one(visit, index, part):
        for way in range(2):
            hop(visit, way, index, part, True).wait_recv()
            if isinstance(index, int) and index == hops - 2:
                final_hop(visit, way, part).start()
            else:
                hop(visit, way, index + 1, part).start()

    def cross(visit, starts=None, work=()):
        depart(visit)
        work = list(work)
        if not work:
            starts = hops - 2

        def step(index, carry):
            for part in range(chunks):
                relay_one(visit, index, part)
            return carry

        if starts > 0:
            lax.fori_loop(0, starts, step, 0)
        for index in range(starts, hops - 1):
            left = (PACE[0] if index == starts else PACE[1]) if work else 0
            for part in range(chunks):
                relay_one(visit, index, part)
                for _ in range(left):
                    if work:
                        work.pop(0)()
        for piece_of_work in work:
            piece_of_work()

    def whole(source, landing, visit, way):
        return pltpu.make_async_remote_copy(
            src_ref=source,
            dst_ref=landing,
            send_sem=far_send.at[visit, way],
            recv_sem=far_recv.at[visit],
            device_id=chip(column, z + 1, 1),
            device_id_type=MESH,
        )

    def landed(visit):
        landing = q_in.at[visit + 1] if visit < VISITS - 1 else items_ref
        whole(q_out.at[visit], landing, visit, 0).wait_recv()

    def drain_far():
        for visit in range(VISITS):
            for way in range(2):
                slots = relay.at[visit, way]
                whole(slots, slots, visit, way).wait_send()

    def gradient_over(other):
        return pltpu.make_async_remote_copy(
            src_ref=g_v,
            dst_ref=g_peer,
            send_sem=g_send,
            recv_sem=g_recv,
            device_id={"user": other},
            device_id_type=MESH,
        )

    parts = runs.shape[3]
    part_rows = share // parts

    def run_copy(who, way, d, part, source, target):
        return pltpu.make_async_remote_copy(
            src_ref=source,
            dst_ref=runs.at[who, way, d, part],
            send_sem=run_send.at[who],
            recv_sem=run_recv.at[who, way, d, part],
            device_id={"isec": target},
            device_id_type=MESH,
        )

    def shard(ref, d, part):
        start = pl.multiple_of(d * share + part * part_rows, part_rows)
        return ref.at[pl.ds(start, part_rows), :]

    def run_step(who, g_ref, way, d, target, inner, outer, sends):
        @pl.when(inner)
        def _():
            for part in range(parts):
                run = runs.at[who, way, d, part]
                run_copy(who, way, d, part, run, s).wait_recv()

                @pl.when(sends)
                def _():
                    run[...] = run[...] + shard(g_ref, d, part)[...]
                    run_copy(who, way, d, part, run, target).start()

        @pl.when(outer & sends)
        def _():
            for part in range(parts):
                run_copy(who, way, d, part, shard(g_ref, d, part), target).start()

    def line_step(who, g_ref, t):
        d = last + s - t

        @pl.when(t >= s)
        def _():
            run_step(who, g_ref, 0, d, s + 1, s > 0, s == 0, d > s)

        b = t - last + s

        @pl.when(t >= last - s)
        def _():
            run_step(who, g_ref, 1, b, s - 1, s < last, s == last, b < s)

    def line_total(who, g_ref, part):
        mine = shard(g_ref, s, part)[...]
        right = jnp.where(s > 0, runs[who, 0, s, part], 0.0)
        left = jnp.where(s < last, runs[who, 1, s, part], 0.0)
        return mine + (right + left)

    def drain_line(who, g_ref):
        sent = g_ref.at[pl.ds(0, last * share), :]
        pltpu.make_async_remote_copy(
            src_ref=sent,
            dst_ref=sent,
            send_sem=run_send.at[who],
            recv_sem=fin_recv,
            device_id={"isec": lax.rem(s + 1, n_isec)},
            device_id_type=MESH,
        ).wait_send()

    def finish(total, part):
        own = shard(p_v, s, part)[...]
        rows = pl.ds(part * part_rows, part_rows)
        users_ref[rows, :] = own - user_rate * (total + shrinkage * own)

    def finish_copy(other):
        return pltpu.make_async_remote_copy(
            src_ref=fin_out,
            dst_ref=fin_in,
            send_sem=fin_send,
            recv_sem=fin_recv,
            device_id={"user": other},
            device_id_type=MESH,
        )

    errors(0)
    item_step(0)

    @pl.when(core == 0)
    def _():
        greeted = jnp.where(s > 0, 1, 0) + jnp.where(s < last, 1, 0)
        pl.semaphore_wait(barrier, 6 + greeted)
        near(0).start()
        user_step(0)
        for visit in range(1, VISITS - 1):
            landed(visit - 1)
            errors(visit)
            item_step(visit)
            near(visit).start()
            user_step(visit)
        gradient_over(prv).wait_recv()

        def first_steps(t, carry):
            line_step(0, g_peer, t)
            return carry

        def both_steps(t, carry):
            line_step(0, g_peer, t)
            line_step(1, g_v, t - LEAD)
            return carry

        def last_steps(t, carry):
            line_step(1, g_v, t)
            return carry

        lax.fori_loop(0, LEAD, first_steps, 0)
        landed(VISITS - 2)
        errors(VISITS - 1)
        user_step(VISITS - 1)
        item_step(VISITS - 1)
        near(VISITS - 1).start()
        lax.fori_loop(LEAD, n_isec, both_steps, 0)
        for part in range(parts):
            rows = pl.ds(part * part_rows, part_rows)
            fin_out[rows, :] = line_total(0, g_peer, part)
        finish_copy(nxt).start()
        lax.fori_loop(n_isec - LEAD, n_isec, last_steps, 0)
        for part in range(parts):
            finish(line_total(1, g_v, part), part)
        drain_line(0, g_peer)
        drain_line(1, g_v)
        finish_copy(nxt).wait_send()
        for visit in range(VISITS):
            near(visit).wait_send()
        landed(VISITS - 1)

    @pl.when(core == 1)
    def _():
        pl.semaphore_wait(barrier, 8)
        first = [functools.partial(user_step_of, 0, i) for i in range(user_tiles)]
        cross(0, 0, first + pieces(1))
        cross(1, STARTS, pieces(2))
        cross(2, STARTS, pieces(3))
        cross(3)
        gradient_over(prv).wait_send()
        finish_copy(nxt).wait_recv()
        for part in range(parts):
            finish(fin_in[pl.ds(part * part_rows, part_rows), :], part)
        drain_far()
        near(VISITS - 1).wait_recv()


def on_device(n_user, n_isec, user_factors, item_factors, confidence, tile_ids, tile_counts):
    user_rows, rank = user_factors.shape
    block = item_factors.shape[0]
    tiles = confidence.shape[3]
    share = user_rows // n_isec
    vmem = functools.partial(pltpu.VMEM, dtype=F32)
    dma = pltpu.SemaphoreType.DMA
    return pl.pallas_call(
        functools.partial(kernel, n_user, n_isec),
        out_shape=(vmem((share, rank)), vmem((block, rank))),
        in_specs=[pl.BlockSpec(memory_space=pl.ANY)] * 5,
        out_specs=(pl.BlockSpec(memory_space=pltpu.VMEM),) * 2,
        scratch_shapes=[
            pltpu.SMEM((VISITS, tiles), jnp.int32),
            pltpu.SMEM((VISITS,), jnp.int32),
            vmem((user_rows, rank)),
            pltpu.VMEM((user_rows, rank), BF16),
            pltpu.VMEM((user_rows, rank), BF16),
            vmem((VISITS, block, rank)),
            vmem((VISITS, block, rank)),
            pltpu.VMEM((block, rank), BF16),
            pltpu.VMEM((block, rank), BF16),
            pltpu.VMEM((VISITS, tiles, TILE, TILE), BF16),
            pltpu.VMEM((block, user_rows), BF16),
            pltpu.VMEM((block, user_rows), BF16),
            pltpu.VMEM((user_rows, block), BF16),
            pltpu.VMEM((user_rows, block), BF16),
            vmem((user_rows, rank)),
            vmem((user_rows, rank)),
            vmem((2, 2, n_isec, PARTS, share // PARTS, rank)),
            vmem((share, rank)),
            vmem((share, rank)),
            vmem((VISITS, 2, n_isec // STRIDE, block // 2, rank)),
            dma((user_rows // TILE + 4,)),
            dma((VISITS,)),
            dma((VISITS,)),
            dma((VISITS, 2)),
            dma((VISITS, 2, n_isec // STRIDE - 1, CHUNKS)),
            dma((VISITS,)),
            dma,
            dma,
            dma((2,)),
            dma((2, 2, n_isec, PARTS)),
            dma,
            dma,
        ],
        compiler_params=pltpu.CompilerParams(
            collective_id=0, has_side_effects=True
        ),
        name="window",
    )(tile_ids[0, 0], tile_counts[0, 0], user_factors, item_factors, confidence[0, 0])


def solution(mesh):
    sizes = dict(mesh.shape)
    return jax.shard_map(
        functools.partial(on_device, sizes["user"], sizes["isec"]),
        mesh=mesh,
        in_specs=(
            P("user", None),
            P(("user", "isec"), None),
            P("user", "isec", None, None, None, None),
            P("user", "isec", None, None),
            P("user", "isec", None),
        ),
        out_specs=(P(("user", "isec"), None), P(("user", "isec"), None)),
        check_vma=False,
    )
```

```python
import functools

import jax
import jax.numpy as jnp
from jax import lax
from jax.experimental import pallas as pl
from jax.experimental.pallas import tpu as pltpu
from jax.sharding import PartitionSpec as P

TILE = 128
VISITS = 4
CHUNKS = 4
PARTS = 2
LEAD = 4
PACE = (2, 2)
STARTS = 2
STRIDE = 1

item_rate = 0.02
user_rate = 0.005
shrinkage = 0.1

MESH = pl.DeviceIdType.MESH
F32 = jnp.float32
BF16 = jnp.bfloat16


def halves(value):
    high = value.astype(BF16)
    low = (value - high.astype(F32)).astype(BF16)
    return high, low


def dot3(left, right, dims):
    one = functools.partial(
        lax.dot_general, dimension_numbers=(dims, ((), ())), preferred_element_type=F32
    )
    return one(left[0], right[0]) + (one(left[0], right[1]) + one(left[1], right[0]))


def kernel(
    n_user, n_isec,
    ids_hbm, counts_hbm, p_hbm, q_hbm, c_hbm,
    users_ref, items_ref,
    ids_ref, counts_ref,
    p_v, p_hi, p_lo, q_in, q_out, q_hi, q_lo, c_v, et_hi, et_lo, e_hi, e_lo,
    g_v, g_peer, runs, fin_out, fin_in, relay,
    load_sem, near_send, near_recv, far_send, hop_recv, far_recv,
    g_send, g_recv, run_send, run_recv, fin_send, fin_recv,
):
    user_rows, rank = p_v.shape
    block = q_in.shape[1]
    user_tiles = user_rows // TILE
    item_tiles = block // TILE
    share = user_rows // n_isec
    last = n_isec - 1

    ring = 2 * n_isec
    chunks = hop_recv.shape[2]
    hops = hop_recv.shape[1] + 1
    stride = n_isec // hops
    chunk_rows = block // 2 // chunks

    u = lax.axis_index("user")
    s = lax.axis_index("isec")
    core = lax.rem(u, 2)
    column = u // 4
    z = lax.rem(u // 2, 2) * n_isec + s
    nxt = lax.rem(u + 1, n_user)
    prv = lax.rem(u + n_user - 1, n_user)
    home = lax.rem(u + n_user - (VISITS - 1), n_user)
    guest = lax.rem(u + VISITS - 1, n_user)
    way_step = (stride, ring - stride)

    def owner(col, z_at, at_core):
        return (col * 2 + z_at // n_isec) * 2 + at_core

    def chip(col, z_at, at_core):
        z_at = lax.rem(z_at, ring)
        return {"user": owner(col, z_at, at_core), "isec": lax.rem(z_at, n_isec)}

    def shift_of(visit):
        return 1 if visit < VISITS - 1 else n_user - (VISITS - 1)

    def relay_target(way, visit):
        source = lax.rem(z + (ring - way_step[way]) * (hops - 1), ring)
        first = owner(column, source, 1)
        return {
            "user": lax.rem(first + shift_of(visit), n_user),
            "isec": lax.rem(source, n_isec),
        }

    def relay_origin(way, visit):
        first = lax.rem(u + n_user - shift_of(visit), n_user)
        return chip(first // 4, z + ring - way_step[way], 1)

    load_q = pltpu.make_async_copy(q_hbm, q_in.at[0], load_sem.at[user_tiles])
    load_c = pltpu.make_async_copy(c_hbm, c_v, load_sem.at[user_tiles + 1])

    def load_p(i):
        rows = pl.ds(i * TILE, TILE)
        return pltpu.make_async_copy(p_hbm.at[rows, :], p_v.at[rows, :], load_sem.at[i])

    load_ids = pltpu.make_async_copy(ids_hbm, ids_ref, load_sem.at[user_tiles + 2])
    load_counts = pltpu.make_async_copy(
        counts_hbm, counts_ref, load_sem.at[user_tiles + 3]
    )

    for i in range(user_tiles):
        load_p(i).start()
    load_ids.start()
    load_counts.start()
    load_q.start()
    load_c.start()

    barrier = pltpu.get_barrier_semaphore()

    def greet(device):
        pl.semaphore_signal(barrier, inc=1, device_id=device, device_id_type=MESH)

    @pl.when(core == 1)
    def _():
        for way in range(2):
            greet(chip(column, z + way_step[way], 1))
            greet(relay_target(way, 0))
            greet(relay_target(way, VISITS - 1))
        greet({"user": prv})
        greet({"user": guest})

    @pl.when(core == 0)
    def _():
        for way in range(2):
            greet(relay_origin(way, 0))
            greet(relay_origin(way, VISITS - 1))
        greet({"user": nxt})
        greet({"user": home})

    @pl.when((core == 0) & (s > 0))
    def _():
        greet({"isec": s - 1})

    @pl.when((core == 0) & (s < last))
    def _():
        greet({"isec": s + 1})

    for i in range(user_tiles):
        load_p(i).wait()
        rows = pl.ds(i * TILE, TILE)
        high, low = halves(p_v[rows, :])
        p_hi[rows, :] = high
        p_lo[rows, :] = low
    load_q.wait()
    load_c.wait()
    load_ids.wait()
    load_counts.wait()

    def split_items(visit):
        high, low = halves(q_in[visit])
        q_hi[...] = high
        q_lo[...] = low

    def errors_of(visit, i):
        rows = pl.ds(i * TILE, TILE)
        x = dot3((p_hi[rows, :], p_lo[rows, :]), (q_hi[...], q_lo[...]), ((1,), (1,)))
        for j in range(item_tiles):
            k = i * item_tiles + j
            place = jnp.int32(0)
            live = jnp.int32(0)
            for n in range(c_v.shape[1]):
                hit = (ids_ref[visit, n] == k) & (n < counts_ref[visit])
                place = place + jnp.where(hit, n, 0)
                live = live + jnp.where(hit, 1, 0)
            columns = slice(j * TILE, (j + 1) * TILE)
            weight = c_v[visit, place].astype(F32)
            e = jnp.where(live > 0, weight * (x[:, columns] - 1.0), 0.0)
            high, low = halves(e)
            e_hi[rows, pl.ds(j * TILE, TILE)] = high
            e_lo[rows, pl.ds(j * TILE, TILE)] = low
            high, low = halves(e.T)
            et_hi[pl.ds(j * TILE, TILE), rows] = high
            et_lo[pl.ds(j * TILE, TILE), rows] = low

    def item_step_of(visit, j):
        rows = pl.ds(j * TILE, TILE)
        d = dot3(
            (et_hi[rows, :], et_lo[rows, :]), (p_hi[...], p_lo[...]), ((1,), (0,))
        )
        q = q_in[visit, rows, :]
        q_out[visit, rows, :] = q - item_rate * (d + shrinkage * q)

    def user_step_of(visit, i):
        rows = pl.ds(i * TILE, TILE)
        g = dot3(
            (e_hi[rows, :], e_lo[rows, :]), (q_hi[...], q_lo[...]), ((1,), (0,))
        )
        if visit == 0:
            g_v[rows, :] = g
        else:
            g_v[rows, :] = g_v[rows, :] + g

    def errors(visit):
        split_items(visit)
        for i in range(user_tiles):
            errors_of(visit, i)

    def item_step(visit):
        for j in range(item_tiles):
            item_step_of(visit, j)

    def user_step(visit):
        for i in range(user_tiles):
            user_step_of(visit, i)

    def pieces(visit):
        work = [lambda: near(visit - 1).wait_recv(), lambda: split_items(visit)]
        work += [functools.partial(errors_of, visit, i) for i in range(user_tiles)]
        users_part = [functools.partial(user_step_of, visit, i) for i in range(user_tiles)]
        items_part = [functools.partial(item_step_of, visit, j) for j in range(item_tiles)]
        if visit < VISITS - 1:
            return work + items_part + users_part
        return work + users_part + [lambda: gradient_over(prv).start()] + items_part

    def near(visit):
        return pltpu.make_async_remote_copy(
            src_ref=q_out.at[visit],
            dst_ref=q_in.at[visit + 1] if visit < VISITS - 1 else items_ref,
            send_sem=near_send.at[visit],
            recv_sem=near_recv.at[visit],
            device_id={"user": nxt if visit < VISITS - 1 else home},
            device_id_type=MESH,
        )

    def piece(way, part):
        return pl.ds(way * chunks * chunk_rows + part * chunk_rows, chunk_rows)

    def hop(visit, way, index, part, arrived=False):
        rows = pl.ds(part * chunk_rows, chunk_rows)
        if arrived:
            source = relay.at[visit, way, index, rows, :]
        elif isinstance(index, int) and index == 0:
            source = q_out.at[visit, piece(way, part), :]
        else:
            source = relay.at[visit, way, index - 1, rows, :]
        return pltpu.make_async_remote_copy(
            src_ref=source,
            dst_ref=relay.at[visit, way, index, rows, :],
            send_sem=far_send.at[visit, way],
            recv_sem=hop_recv.at[visit, index, part],
            device_id=chip(column, z + way_step[way], 1),
            device_id_type=MESH,
        )

    def final_hop(visit, way, part):
        rows = pl.ds(part * chunk_rows, chunk_rows)
        landing = q_in.at[visit + 1] if visit < VISITS - 1 else items_ref
        return pltpu.make_async_remote_copy(
            src_ref=relay.at[visit, way, hops - 2, rows, :],
            dst_ref=landing.at[piece(way, part), :],
            send_sem=far_send.at[visit, way],
            recv_sem=far_recv.at[visit],
            device_id=relay_target(way, visit),
            device_id_type=MESH,
        )

    def depart(visit):
        for part in range(chunks):
            for way in range(2):
                hop(visit, way, 0, part).start()

    def relay_one(visit, index, part):
        both = relay.at[visit, :, index, pl.ds(part * chunk_rows, chunk_rows), :]
        pltpu.make_async_remote_copy(
            src_ref=both,
            dst_ref=both,
            send_sem=far_send.at[visit, 0],
            recv_sem=hop_recv.at[visit, index, part],
            device_id=chip(column, z + 1, 1),
            device_id_type=MESH,
        ).wait_recv()
        for way in range(2):
            if isinstance(index, int) and index == hops - 2:
                final_hop(visit, way, part).start()
            else:
                hop(visit, way, index + 1, part).start()

    def cross(visit, starts=None, work=()):
        depart(visit)
        work = list(work)
        if not work:
            starts = hops - 2

        def step(index, carry):
            for part in range(chunks):
                relay_one(visit, index, part)
            return carry

        if starts > 0:
            lax.fori_loop(0, starts, step, 0)
        for index in range(starts, hops - 1):
            left = (PACE[0] if index == starts else PACE[1]) if work else 0
            for part in range(chunks):
                relay_one(visit, index, part)
                for _ in range(left):
                    if work:
                        work.pop(0)()
        for piece_of_work in work:
            piece_of_work()

    def whole(source, landing, visit, way):
        return pltpu.make_async_remote_copy(
            src_ref=source,
            dst_ref=landing,
            send_sem=far_send.at[visit, way],
            recv_sem=far_recv.at[visit],
            device_id=chip(column, z + 1, 1),
            device_id_type=MESH,
        )

    def landed(visit):
        landing = q_in.at[visit + 1] if visit < VISITS - 1 else items_ref
        whole(q_out.at[visit], landing, visit, 0).wait_recv()

    def drain_far():
        for visit in range(VISITS):
            for way in range(2):
                slots = relay.at[visit, way]
                whole(slots, slots, visit, way).wait_send()

    def gradient_over(other):
        return pltpu.make_async_remote_copy(
            src_ref=g_v,
            dst_ref=g_peer,
            send_sem=g_send,
            recv_sem=g_recv,
            device_id={"user": other},
            device_id_type=MESH,
        )

    parts = runs.shape[3]
    part_rows = share // parts

    def run_copy(who, way, d, part, source, target):
        return pltpu.make_async_remote_copy(
            src_ref=source,
            dst_ref=runs.at[who, way, d, part],
            send_sem=run_send.at[who],
            recv_sem=run_recv.at[who, way, d, part],
            device_id={"isec": target},
            device_id_type=MESH,
        )

    def shard(ref, d, part):
        start = pl.multiple_of(d * share + part * part_rows, part_rows)
        return ref.at[pl.ds(start, part_rows), :]

    def run_step(who, g_ref, way, d, part, target, inner, outer, sends):
        run = runs.at[who, way, d, part]

        @pl.when(inner)
        def _():
            run_copy(who, way, d, part, run, s).wait_recv()

            @pl.when(sends)
            def _():
                run[...] = run[...] + shard(g_ref, d, part)[...]
                run_copy(who, way, d, part, run, target).start()

        @pl.when(outer & sends)
        def _():
            run_copy(who, way, d, part, shard(g_ref, d, part), target).start()

    def line_step(who, g_ref, t, part):
        d = last + s - t

        @pl.when(t >= s)
        def _():
            run_step(who, g_ref, 0, d, part, s + 1, s > 0, s == 0, d > s)

        b = t - last + s

        @pl.when(t >= last - s)
        def _():
            run_step(who, g_ref, 1, b, part, s - 1, s < last, s == last, b < s)

    def line_total(who, g_ref, part):
        mine = shard(g_ref, s, part)[...]
        right = jnp.where(s > 0, runs[who, 0, s, part], 0.0)
        left = jnp.where(s < last, runs[who, 1, s, part], 0.0)
        return mine + (right + left)

    def drain_line(who, g_ref):
        sent = g_ref.at[pl.ds(0, last * share), :]
        pltpu.make_async_remote_copy(
            src_ref=sent,
            dst_ref=sent,
            send_sem=run_send.at[who],
            recv_sem=fin_recv,
            device_id={"isec": lax.rem(s + 1, n_isec)},
            device_id_type=MESH,
        ).wait_send()

    def finish(total, part):
        own = shard(p_v, s, part)[...]
        rows = pl.ds(part * part_rows, part_rows)
        users_ref[rows, :] = own - user_rate * (total + shrinkage * own)

    def finish_copy(other):
        return pltpu.make_async_remote_copy(
            src_ref=fin_out,
            dst_ref=fin_in,
            send_sem=fin_send,
            recv_sem=fin_recv,
            device_id={"user": other},
            device_id_type=MESH,
        )

    errors(0)
    item_step(0)

    @pl.when(core == 0)
    def _():
        greeted = jnp.where(s > 0, 1, 0) + jnp.where(s < last, 1, 0)
        pl.semaphore_wait(barrier, 6 + greeted)
        near(0).start()
        user_step(0)
        for visit in range(1, VISITS - 1):
            landed(visit - 1)
            errors(visit)
            item_step(visit)
            near(visit).start()
            user_step(visit)
        gradient_over(prv).wait_recv()

        def first_steps(t, carry):
            for part in range(parts):
                line_step(0, g_peer, t, part)
            return carry

        def both_steps(t, carry):
            for part in range(parts):
                line_step(0, g_peer, t, part)
                line_step(1, g_v, t - LEAD, part)
            return carry

        def last_steps(t, carry):
            for part in range(parts):
                line_step(1, g_v, t, part)
            return carry

        lax.fori_loop(0, LEAD, first_steps, 0)
        landed(VISITS - 2)
        errors(VISITS - 1)
        user_step(VISITS - 1)
        item_step(VISITS - 1)
        near(VISITS - 1).start()
        lax.fori_loop(LEAD, n_isec, both_steps, 0)
        for part in range(parts):
            rows = pl.ds(part * part_rows, part_rows)
            fin_out[rows, :] = line_total(0, g_peer, part)
        finish_copy(nxt).start()
        lax.fori_loop(n_isec - LEAD, n_isec, last_steps, 0)
        for part in range(parts):
            finish(line_total(1, g_v, part), part)
        drain_line(0, g_peer)
        drain_line(1, g_v)
        finish_copy(nxt).wait_send()
        for visit in range(VISITS):
            near(visit).wait_send()
        landed(VISITS - 1)

    @pl.when(core == 1)
    def _():
        pl.semaphore_wait(barrier, 8)
        first = [functools.partial(user_step_of, 0, i) for i in range(user_tiles)]
        cross(0, 0, first + pieces(1))
        cross(1, STARTS, pieces(2))
        cross(2, STARTS, pieces(3))
        cross(3)
        gradient_over(prv).wait_send()
        finish_copy(nxt).wait_recv()
        for part in range(parts):
            finish(fin_in[pl.ds(part * part_rows, part_rows), :], part)
        drain_far()
        near(VISITS - 1).wait_recv()


def on_device(n_user, n_isec, user_factors, item_factors, confidence, tile_ids, tile_counts):
    user_rows, rank = user_factors.shape
    block = item_factors.shape[0]
    tiles = confidence.shape[3]
    share = user_rows // n_isec
    vmem = functools.partial(pltpu.VMEM, dtype=F32)
    dma = pltpu.SemaphoreType.DMA
    return pl.pallas_call(
        functools.partial(kernel, n_user, n_isec),
        out_shape=(vmem((share, rank)), vmem((block, rank))),
        in_specs=[pl.BlockSpec(memory_space=pl.ANY)] * 5,
        out_specs=(pl.BlockSpec(memory_space=pltpu.VMEM),) * 2,
        scratch_shapes=[
            pltpu.SMEM((VISITS, tiles), jnp.int32),
            pltpu.SMEM((VISITS,), jnp.int32),
            vmem((user_rows, rank)),
            pltpu.VMEM((user_rows, rank), BF16),
            pltpu.VMEM((user_rows, rank), BF16),
            vmem((VISITS, block, rank)),
            vmem((VISITS, block, rank)),
            pltpu.VMEM((block, rank), BF16),
            pltpu.VMEM((block, rank), BF16),
            pltpu.VMEM((VISITS, tiles, TILE, TILE), BF16),
            pltpu.VMEM((block, user_rows), BF16),
            pltpu.VMEM((block, user_rows), BF16),
            pltpu.VMEM((user_rows, block), BF16),
            pltpu.VMEM((user_rows, block), BF16),
            vmem((user_rows, rank)),
            vmem((user_rows, rank)),
            vmem((2, 2, n_isec, PARTS, share // PARTS, rank)),
            vmem((share, rank)),
            vmem((share, rank)),
            vmem((VISITS, 2, n_isec // STRIDE, block // 2, rank)),
            dma((user_rows // TILE + 4,)),
            dma((VISITS,)),
            dma((VISITS,)),
            dma((VISITS, 2)),
            dma((VISITS, n_isec // STRIDE - 1, CHUNKS)),
            dma((VISITS,)),
            dma,
            dma,
            dma((2,)),
            dma((2, 2, n_isec, PARTS)),
            dma,
            dma,
        ],
        compiler_params=pltpu.CompilerParams(
            collective_id=0, has_side_effects=True
        ),
        name="window",
    )(tile_ids[0, 0], tile_counts[0, 0], user_factors, item_factors, confidence[0, 0])


def solution(mesh):
    sizes = dict(mesh.shape)
    return jax.shard_map(
        functools.partial(on_device, sizes["user"], sizes["isec"]),
        mesh=mesh,
        in_specs=(
            P("user", None),
            P(("user", "isec"), None),
            P("user", "isec", None, None, None, None),
            P("user", "isec", None, None),
            P("user", "isec", None),
        ),
        out_specs=(P(("user", "isec"), None), P(("user", "isec"), None)),
        check_vma=False,
    )
```

```python
import functools

import jax
import jax.numpy as jnp
from jax import lax
from jax.experimental import pallas as pl
from jax.experimental.pallas import tpu as pltpu
from jax.sharding import PartitionSpec as P

TILE = 128
VISITS = 4
CHUNKS = 4
PARTS = 2
LEAD = 4
PACE = (1, 2)
STARTS = 2
STRIDE = 1

item_rate = 0.02
user_rate = 0.005
shrinkage = 0.1

MESH = pl.DeviceIdType.MESH
F32 = jnp.float32
BF16 = jnp.bfloat16


def halves(value):
    high = value.astype(BF16)
    low = (value - high.astype(F32)).astype(BF16)
    return high, low


def dot3(left, right, dims):
    one = functools.partial(
        lax.dot_general, dimension_numbers=(dims, ((), ())), preferred_element_type=F32
    )
    return one(left[0], right[0]) + (one(left[0], right[1]) + one(left[1], right[0]))


def kernel(
    n_user, n_isec,
    ids_hbm, counts_hbm, p_hbm, q_hbm, c_hbm,
    users_ref, items_ref,
    ids_ref, counts_ref,
    p_v, p_hi, p_lo, q_in, q_out, q_hi, q_lo, c_v, et_hi, et_lo, e_hi, e_lo,
    g_v, g_peer, runs, fin_out, fin_in, relay,
    load_sem, near_send, near_recv, far_send, hop_recv, far_recv,
    g_send, g_recv, run_send, run_recv, fin_send, fin_recv,
):
    user_rows, rank = p_v.shape
    block = q_in.shape[1]
    user_tiles = user_rows // TILE
    item_tiles = block // TILE
    share = user_rows // n_isec
    last = n_isec - 1

    ring = 2 * n_isec
    chunks = hop_recv.shape[2]
    hops = hop_recv.shape[1] + 1
    stride = n_isec // hops
    chunk_rows = block // 2 // chunks

    u = lax.axis_index("user")
    s = lax.axis_index("isec")
    core = lax.rem(u, 2)
    column = u // 4
    z = lax.rem(u // 2, 2) * n_isec + s
    nxt = lax.rem(u + 1, n_user)
    prv = lax.rem(u + n_user - 1, n_user)
    home = lax.rem(u + n_user - (VISITS - 1), n_user)
    guest = lax.rem(u + VISITS - 1, n_user)
    way_step = (stride, ring - stride)

    def owner(col, z_at, at_core):
        return (col * 2 + z_at // n_isec) * 2 + at_core

    def chip(col, z_at, at_core):
        z_at = lax.rem(z_at, ring)
        return {"user": owner(col, z_at, at_core), "isec": lax.rem(z_at, n_isec)}

    def shift_of(visit):
        return 1 if visit < VISITS - 1 else n_user - (VISITS - 1)

    def relay_target(way, visit):
        source = lax.rem(z + (ring - way_step[way]) * (hops - 1), ring)
        first = owner(column, source, 1)
        return {
            "user": lax.rem(first + shift_of(visit), n_user),
            "isec": lax.rem(source, n_isec),
        }

    def relay_origin(way, visit):
        first = lax.rem(u + n_user - shift_of(visit), n_user)
        return chip(first // 4, z + ring - way_step[way], 1)

    load_q = pltpu.make_async_copy(q_hbm, q_in.at[0], load_sem.at[user_tiles])
    load_c = pltpu.make_async_copy(c_hbm, c_v, load_sem.at[user_tiles + 1])

    def load_p(i):
        rows = pl.ds(i * TILE, TILE)
        return pltpu.make_async_copy(p_hbm.at[rows, :], p_v.at[rows, :], load_sem.at[i])

    load_ids = pltpu.make_async_copy(ids_hbm, ids_ref, load_sem.at[user_tiles + 2])
    load_counts = pltpu.make_async_copy(
        counts_hbm, counts_ref, load_sem.at[user_tiles + 3]
    )

    for i in range(user_tiles):
        load_p(i).start()
    load_ids.start()
    load_counts.start()
    load_q.start()
    load_c.start()

    barrier = pltpu.get_barrier_semaphore()

    def greet(device):
        pl.semaphore_signal(barrier, inc=1, device_id=device, device_id_type=MESH)

    @pl.when(core == 1)
    def _():
        for way in range(2):
            greet(chip(column, z + way_step[way], 1))
            greet(relay_target(way, 0))
            greet(relay_target(way, VISITS - 1))
        greet({"user": prv})
        greet({"user": guest})

    @pl.when(core == 0)
    def _():
        for way in range(2):
            greet(relay_origin(way, 0))
            greet(relay_origin(way, VISITS - 1))
        greet({"user": nxt})
        greet({"user": home})

    @pl.when((core == 0) & (s > 0))
    def _():
        greet({"isec": s - 1})

    @pl.when((core == 0) & (s < last))
    def _():
        greet({"isec": s + 1})

    for i in range(user_tiles):
        load_p(i).wait()
        rows = pl.ds(i * TILE, TILE)
        high, low = halves(p_v[rows, :])
        p_hi[rows, :] = high
        p_lo[rows, :] = low
    load_q.wait()
    load_c.wait()
    load_ids.wait()
    load_counts.wait()

    def split_items(visit):
        high, low = halves(q_in[visit])
        q_hi[...] = high
        q_lo[...] = low

    def errors_of(visit, i):
        rows = pl.ds(i * TILE, TILE)
        x = dot3((p_hi[rows, :], p_lo[rows, :]), (q_hi[...], q_lo[...]), ((1,), (1,)))
        for j in range(item_tiles):
            k = i * item_tiles + j
            place = jnp.int32(0)
            live = jnp.int32(0)
            for n in range(c_v.shape[1]):
                hit = (ids_ref[visit, n] == k) & (n < counts_ref[visit])
                place = place + jnp.where(hit, n, 0)
                live = live + jnp.where(hit, 1, 0)
            columns = slice(j * TILE, (j + 1) * TILE)
            weight = c_v[visit, place].astype(F32)
            e = jnp.where(live > 0, weight * (x[:, columns] - 1.0), 0.0)
            high, low = halves(e)
            e_hi[rows, pl.ds(j * TILE, TILE)] = high
            e_lo[rows, pl.ds(j * TILE, TILE)] = low
            high, low = halves(e.T)
            et_hi[pl.ds(j * TILE, TILE), rows] = high
            et_lo[pl.ds(j * TILE, TILE), rows] = low

    def item_step_of(visit, j):
        rows = pl.ds(j * TILE, TILE)
        d = dot3(
            (et_hi[rows, :], et_lo[rows, :]), (p_hi[...], p_lo[...]), ((1,), (0,))
        )
        q = q_in[visit, rows, :]
        q_out[visit, rows, :] = q - item_rate * (d + shrinkage * q)

    def user_step_of(visit, i):
        rows = pl.ds(i * TILE, TILE)
        g = dot3(
            (e_hi[rows, :], e_lo[rows, :]), (q_hi[...], q_lo[...]), ((1,), (0,))
        )
        if visit == 0:
            g_v[rows, :] = g
        else:
            g_v[rows, :] = g_v[rows, :] + g

    def errors(visit):
        split_items(visit)
        for i in range(user_tiles):
            errors_of(visit, i)

    def item_step(visit):
        for j in range(item_tiles):
            item_step_of(visit, j)

    def user_step(visit):
        for i in range(user_tiles):
            user_step_of(visit, i)

    def pieces(visit):
        work = [lambda: near(visit - 1).wait_recv(), lambda: split_items(visit)]
        work += [functools.partial(errors_of, visit, i) for i in range(user_tiles)]
        users_part = [functools.partial(user_step_of, visit, i) for i in range(user_tiles)]
        items_part = [functools.partial(item_step_of, visit, j) for j in range(item_tiles)]
        if visit < VISITS - 1:
            return work + items_part + users_part
        return work + users_part + [lambda: gradient_over(prv).start()] + items_part

    def near(visit):
        return pltpu.make_async_remote_copy(
            src_ref=q_out.at[visit],
            dst_ref=q_in.at[visit + 1] if visit < VISITS - 1 else items_ref,
            send_sem=near_send.at[visit],
            recv_sem=near_recv.at[visit],
            device_id={"user": nxt if visit < VISITS - 1 else home},
            device_id_type=MESH,
        )

    def piece(way, part):
        return pl.ds(way * chunks * chunk_rows + part * chunk_rows, chunk_rows)

    def hop(visit, way, index, part, arrived=False):
        rows = pl.ds(part * chunk_rows, chunk_rows)
        if arrived:
            source = relay.at[visit, way, index, rows, :]
        elif isinstance(index, int) and index == 0:
            source = q_out.at[visit, piece(way, part), :]
        else:
            source = relay.at[visit, way, index - 1, rows, :]
        return pltpu.make_async_remote_copy(
            src_ref=source,
            dst_ref=relay.at[visit, way, index, rows, :],
            send_sem=far_send.at[visit, way],
            recv_sem=hop_recv.at[visit, index, part],
            device_id=chip(column, z + way_step[way], 1),
            device_id_type=MESH,
        )

    def final_hop(visit, way, part):
        rows = pl.ds(part * chunk_rows, chunk_rows)
        landing = q_in.at[visit + 1] if visit < VISITS - 1 else items_ref
        return pltpu.make_async_remote_copy(
            src_ref=relay.at[visit, way, hops - 2, rows, :],
            dst_ref=landing.at[piece(way, part), :],
            send_sem=far_send.at[visit, way],
            recv_sem=far_recv.at[visit],
            device_id=relay_target(way, visit),
            device_id_type=MESH,
        )

    def depart(visit):
        for part in range(chunks):
            for way in range(2):
                hop(visit, way, 0, part).start()

    def relay_one(visit, index, part):
        both = relay.at[visit, :, index, pl.ds(part * chunk_rows, chunk_rows), :]
        pltpu.make_async_remote_copy(
            src_ref=both,
            dst_ref=both,
            send_sem=far_send.at[visit, 0],
            recv_sem=hop_recv.at[visit, index, part],
            device_id=chip(column, z + 1, 1),
            device_id_type=MESH,
        ).wait_recv()
        for way in range(2):
            if isinstance(index, int) and index == hops - 2:
                final_hop(visit, way, part).start()
            else:
                hop(visit, way, index + 1, part).start()

    def cross(visit, starts=None, work=()):
        depart(visit)
        work = list(work)
        if not work:
            starts = hops - 2

        def step(index, carry):
            for part in range(chunks):
                relay_one(visit, index, part)
            return carry

        if starts > 0:
            lax.fori_loop(0, starts, step, 0)
        for index in range(starts, hops - 1):
            left = (PACE[0] if index == starts else PACE[1]) if work else 0
            for part in range(chunks):
                relay_one(visit, index, part)
                for _ in range(left):
                    if work:
                        work.pop(0)()
        for piece_of_work in work:
            piece_of_work()

    def whole(source, landing, visit, way):
        return pltpu.make_async_remote_copy(
            src_ref=source,
            dst_ref=landing,
            send_sem=far_send.at[visit, way],
            recv_sem=far_recv.at[visit],
            device_id=chip(column, z + 1, 1),
            device_id_type=MESH,
        )

    def landed(visit):
        landing = q_in.at[visit + 1] if visit < VISITS - 1 else items_ref
        whole(q_out.at[visit], landing, visit, 0).wait_recv()

    def drain_far():
        for visit in range(VISITS):
            for way in range(2):
                slots = relay.at[visit, way]
                whole(slots, slots, visit, way).wait_send()

    def gradient_over(other):
        return pltpu.make_async_remote_copy(
            src_ref=g_v,
            dst_ref=g_peer,
            send_sem=g_send,
            recv_sem=g_recv,
            device_id={"user": other},
            device_id_type=MESH,
        )

    parts = runs.shape[3]
    part_rows = share // parts

    def run_copy(who, way, d, part, source, target):
        return pltpu.make_async_remote_copy(
            src_ref=source,
            dst_ref=runs.at[who, way, d, part],
            send_sem=run_send.at[who],
            recv_sem=run_recv.at[who, way, d, part],
            device_id={"isec": target},
            device_id_type=MESH,
        )

    def shard(ref, d, part):
        start = pl.multiple_of(d * share + part * part_rows, part_rows)
        return ref.at[pl.ds(start, part_rows), :]

    def run_step(who, g_ref, way, d, part, target, inner, outer, sends):
        run = runs.at[who, way, d, part]

        @pl.when(inner)
        def _():
            run_copy(who, way, d, part, run, s).wait_recv()

            @pl.when(sends)
            def _():
                run[...] = run[...] + shard(g_ref, d, part)[...]
                run_copy(who, way, d, part, run, target).start()

        @pl.when(outer & sends)
        def _():
            run_copy(who, way, d, part, shard(g_ref, d, part), target).start()

    def line_step(who, g_ref, t, part):
        d = last + s - t

        @pl.when(t >= s)
        def _():
            run_step(who, g_ref, 0, d, part, s + 1, s > 0, s == 0, d > s)

        b = t - last + s

        @pl.when(t >= last - s)
        def _():
            run_step(who, g_ref, 1, b, part, s - 1, s < last, s == last, b < s)

    def line_total(who, g_ref, part):
        mine = shard(g_ref, s, part)[...]
        right = jnp.where(s > 0, runs[who, 0, s, part], 0.0)
        left = jnp.where(s < last, runs[who, 1, s, part], 0.0)
        return mine + (right + left)

    def drain_line(who, g_ref):
        sent = g_ref.at[pl.ds(0, last * share), :]
        pltpu.make_async_remote_copy(
            src_ref=sent,
            dst_ref=sent,
            send_sem=run_send.at[who],
            recv_sem=fin_recv,
            device_id={"isec": lax.rem(s + 1, n_isec)},
            device_id_type=MESH,
        ).wait_send()

    def finish(total, part):
        own = shard(p_v, s, part)[...]
        rows = pl.ds(part * part_rows, part_rows)
        users_ref[rows, :] = own - user_rate * (total + shrinkage * own)

    def finish_copy(other):
        return pltpu.make_async_remote_copy(
            src_ref=fin_out,
            dst_ref=fin_in,
            send_sem=fin_send,
            recv_sem=fin_recv,
            device_id={"user": other},
            device_id_type=MESH,
        )

    errors(0)
    item_step(0)

    @pl.when(core == 0)
    def _():
        greeted = jnp.where(s > 0, 1, 0) + jnp.where(s < last, 1, 0)
        pl.semaphore_wait(barrier, 6 + greeted)
        near(0).start()
        user_step(0)
        for visit in range(1, VISITS - 1):
            landed(visit - 1)
            errors(visit)
            item_step(visit)
            near(visit).start()
            user_step(visit)
        gradient_over(prv).wait_recv()

        def first_steps(t, carry):
            for part in range(parts):
                line_step(0, g_peer, t, part)
            return carry

        def both_steps(t, carry):
            for part in range(parts):
                line_step(0, g_peer, t, part)
                line_step(1, g_v, t - LEAD, part)
            return carry

        def last_steps(t, carry):
            for part in range(parts):
                line_step(1, g_v, t, part)
            return carry

        lax.fori_loop(0, LEAD, first_steps, 0)
        landed(VISITS - 2)
        errors(VISITS - 1)
        user_step(VISITS - 1)
        item_step(VISITS - 1)
        near(VISITS - 1).start()
        lax.fori_loop(LEAD, n_isec, both_steps, 0)
        for part in range(parts):
            rows = pl.ds(part * part_rows, part_rows)
            fin_out[rows, :] = line_total(0, g_peer, part)
        finish_copy(nxt).start()
        lax.fori_loop(n_isec - LEAD, n_isec, last_steps, 0)
        for part in range(parts):
            finish(line_total(1, g_v, part), part)
        drain_line(0, g_peer)
        drain_line(1, g_v)
        finish_copy(nxt).wait_send()
        for visit in range(VISITS):
            near(visit).wait_send()
        landed(VISITS - 1)

    @pl.when(core == 1)
    def _():
        pl.semaphore_wait(barrier, 8)
        first = [functools.partial(user_step_of, 0, i) for i in range(user_tiles)]
        cross(0, 0, first + pieces(1))
        cross(1, STARTS, pieces(2))
        cross(2, STARTS, pieces(3))
        cross(3)
        gradient_over(prv).wait_send()
        finish_copy(nxt).wait_recv()
        for part in range(parts):
            finish(fin_in[pl.ds(part * part_rows, part_rows), :], part)
        drain_far()
        near(VISITS - 1).wait_recv()


def on_device(n_user, n_isec, user_factors, item_factors, confidence, tile_ids, tile_counts):
    user_rows, rank = user_factors.shape
    block = item_factors.shape[0]
    tiles = confidence.shape[3]
    share = user_rows // n_isec
    vmem = functools.partial(pltpu.VMEM, dtype=F32)
    dma = pltpu.SemaphoreType.DMA
    return pl.pallas_call(
        functools.partial(kernel, n_user, n_isec),
        out_shape=(vmem((share, rank)), vmem((block, rank))),
        in_specs=[pl.BlockSpec(memory_space=pl.ANY)] * 5,
        out_specs=(pl.BlockSpec(memory_space=pltpu.VMEM),) * 2,
        scratch_shapes=[
            pltpu.SMEM((VISITS, tiles), jnp.int32),
            pltpu.SMEM((VISITS,), jnp.int32),
            vmem((user_rows, rank)),
            pltpu.VMEM((user_rows, rank), BF16),
            pltpu.VMEM((user_rows, rank), BF16),
            vmem((VISITS, block, rank)),
            vmem((VISITS, block, rank)),
            pltpu.VMEM((block, rank), BF16),
            pltpu.VMEM((block, rank), BF16),
            pltpu.VMEM((VISITS, tiles, TILE, TILE), BF16),
            pltpu.VMEM((block, user_rows), BF16),
            pltpu.VMEM((block, user_rows), BF16),
            pltpu.VMEM((user_rows, block), BF16),
            pltpu.VMEM((user_rows, block), BF16),
            vmem((user_rows, rank)),
            vmem((user_rows, rank)),
            vmem((2, 2, n_isec, PARTS, share // PARTS, rank)),
            vmem((share, rank)),
            vmem((share, rank)),
            vmem((VISITS, 2, n_isec // STRIDE, block // 2, rank)),
            dma((user_rows // TILE + 4,)),
            dma((VISITS,)),
            dma((VISITS,)),
            dma((VISITS, 2)),
            dma((VISITS, n_isec // STRIDE - 1, CHUNKS)),
            dma((VISITS,)),
            dma,
            dma,
            dma((2,)),
            dma((2, 2, n_isec, PARTS)),
            dma,
            dma,
        ],
        compiler_params=pltpu.CompilerParams(
            collective_id=0, has_side_effects=True
        ),
        name="window",
    )(tile_ids[0, 0], tile_counts[0, 0], user_factors, item_factors, confidence[0, 0])


def solution(mesh):
    sizes = dict(mesh.shape)
    return jax.shard_map(
        functools.partial(on_device, sizes["user"], sizes["isec"]),
        mesh=mesh,
        in_specs=(
            P("user", None),
            P(("user", "isec"), None),
            P("user", "isec", None, None, None, None),
            P("user", "isec", None, None),
            P("user", "isec", None),
        ),
        out_specs=(P(("user", "isec"), None), P(("user", "isec"), None)),
        check_vma=False,
    )
```
